256 devices in a mesh: ctx: 128 (over z, x, y), pb: 2 (over core).
Axes of the slice: x: 4, y: 4, z: 8, core: 2. Of those that a mesh axis runs over, the one named last changes fastest.
Arguments:
- queries: bfloat16 [64, 512, 2048], P('pb', 'ctx'), may hold values from -100 to 100
- key_blocks: bfloat16 [512, 512, 512], P('ctx'), may hold values from -12 to 12
- value_blocks: bfloat16 [512, 512, 512], P('ctx'), may hold values from -6 to 6
- selected: int32 [64, 3], replicated, may hold values from 0 to 447, as said below
Outputs:
- attended: bfloat16 [64, 512, 2048], P('pb', 'ctx')
The draws below stay inside these ranges and needn't reach their ends.
Inputs may be any that keep to these rules, and one draw needn't show every extreme that they name: `selected`: row b names 3 different KV blocks, all before block 448. Query blocks b < 32 form pb group 0, the others group 1. Counting own blocks too, the KV blocks kept by one ctx index are named by query blocks of one pb group only, and at most 4 times in all; some ctx index is named exactly 4 times.
All inputs are finite; a program needn't handle non-finite values.
Results may differ from the reference program's by a relative error of at most 0.0051.
Values may be sent and summed in bfloat16 or wider, within the bound.
No kernel may reach another device: no remote copies, remote signals or barrier semaphores. Data moves between devices by JAX's collectives and lax.ppermute only.
A program may use at most 192 MiB of HBM per device.

```python
import math
import jax
import jax.numpy as jnp
import numpy as np
from jax import lax

G = 4
HQ = 4
HD = 128
BLOCK = 512
TOPK = 3
KVB_DEV = 4
MOST = 4
NQB = 64
NKB = 512


def key_block(base_key, block_id):
    sub_key = jax.random.fold_in(jax.random.fold_in(base_key, 7001), block_id)
    base_draw = jnp.clip(jax.random.normal(jax.random.fold_in(sub_key, 1), (BLOCK, G * HD), jnp.float32), -4.0, 4.0)
    row_scale = jnp.exp(jax.random.uniform(jax.random.fold_in(sub_key, 2), (BLOCK, 1), jnp.float32, math.log(0.3), math.log(3.0)))
    return base_draw * row_scale


def draw_key_blocks(key, part):

    def single_block(block_id):
        return key_block(key, block_id)
    return jax.vmap(single_block)(jnp.arange(NKB, dtype=jnp.int32)).astype(jnp.bfloat16)


def draw_queries(key, part):
    sub_key = jax.random.fold_in(key, 7002)
    base_draw = jnp.clip(jax.random.normal(sub_key, (NQB, BLOCK, G * HQ * HD), jnp.float32), -5.0, 5.0)
    return base_draw.astype(jnp.bfloat16)


def draw_selected(key, part):
    half_blocks = NQB // 2
    entries = TOPK * half_blocks
    hot_count = entries // 8
    remainder = entries - MOST * hot_count
    pair_count = remainder // 2
    single_count = remainder - 2 * pair_count
    used_owners = hot_count + pair_count + single_count
    ranks = np.concatenate([np.repeat(np.arange(hot_count), MOST), np.repeat(np.arange(pair_count) + hot_count, 2), np.arange(single_count) + hot_count + pair_count]).astype(np.int32)
    prefix_owners = (NKB - NQB) // KVB_DEV
    shuffled = jax.random.permutation(jax.random.fold_in(key, 7101), prefix_owners).astype(jnp.int32)
    group_rows = []
    for group_idx in range(2):
        owner_list = shuffled[group_idx * used_owners + jnp.asarray(ranks)]
        inner = jax.random.randint(jax.random.fold_in(key, 7102 + group_idx), (entries,), 0, KVB_DEV).astype(jnp.int32)
        chosen = (owner_list * KVB_DEV + inner).reshape(TOPK, half_blocks).T
        order = jax.random.permutation(jax.random.fold_in(key, 7104 + group_idx), half_blocks)
        group_rows.append(chosen[order])
    return jnp.concatenate(group_rows, axis=0).astype(jnp.int32)


def block_levels(own_key, extent, shards, smallest, largest):
    gain, own = 1.0, jax.random.fold_in(own_key, 6)
    for dim, blocks in shards:
        heights = jnp.exp(jax.random.uniform(jax.random.fold_in(own, dim), (blocks,), jnp.float32, smallest / len(shards), largest / len(shards)))
        gain = gain * jnp.repeat(heights, extent[dim] // blocks).reshape([-1 if axis == dim else 1 for axis in range(len(extent))])
    return gain


def gaussian(key, extent, deviation, most, pieces=(), kind=jnp.bfloat16):
    level = block_levels(key, extent, pieces, -0.22, 0.18) if pieces else 1.0
    values = jax.random.normal(key, extent, jnp.float32) * deviation * level
    return jnp.minimum(jnp.maximum(values, -most), most).astype(kind)


def setup_inputs(seed: int = 0) -> dict:
    seeds = jax.random.split(jax.random.key(seed), 5)
    queries = draw_queries(jax.random.fold_in(seeds[4], 71), 0)
    key_blocks = draw_key_blocks(jax.random.fold_in(seeds[4], 71), 0)
    value_blocks = gaussian(seeds[2], (NKB, BLOCK, G * HD), 1.0, 6.0, ((0, 128),))
    selected = draw_selected(jax.random.fold_in(seeds[4], 71), 0)
    return dict(queries=queries, key_blocks=key_blocks, value_blocks=value_blocks, selected=selected)


def partial_block(q_rows, k_blk, v_blk, positions, is_causal):
    row_count = q_rows.shape[0]
    q_heads = q_rows.reshape(row_count, G, HQ, HD).astype(jnp.float32)
    k_heads = k_blk.reshape(BLOCK, G, HD).astype(jnp.float32)
    v_heads = v_blk.reshape(BLOCK, G, HD).astype(jnp.float32)
    scores = jnp.einsum('rghd,kgd->ghrk', q_heads, k_heads) * (1.0 / math.sqrt(HD))
    key_pos = jnp.arange(BLOCK, dtype=jnp.int32)
    allowed = jnp.logical_or(key_pos[None, :] <= positions[:, None], jnp.logical_not(is_causal))
    scores = jnp.where(allowed, scores, -jnp.inf)
    block_max = lax.optimization_barrier(jnp.max(scores, axis=-1))
    weights = jnp.exp(scores - block_max[..., None]).astype(jnp.bfloat16)
    block_sum = lax.optimization_barrier(jnp.sum(weights.astype(jnp.float32), axis=-1))
    partial_value = jnp.einsum('ghrk,kgd->rghd', weights.astype(jnp.float32), v_heads)
    partial_value = partial_value / jnp.transpose(block_sum, (2, 0, 1))[..., None]
    return (partial_value.astype(jnp.bfloat16).reshape(row_count, G * HQ * HD), jnp.transpose(block_max, (2, 0, 1)).reshape(row_count, G * HQ), jnp.transpose(block_sum, (2, 0, 1)).reshape(row_count, G * HQ))

def reference(queries, key_blocks, value_blocks, selected):
    positions = jnp.arange(BLOCK, dtype=jnp.int32)

    def one_query_block(block_index):
        q_rows = lax.dynamic_index_in_dim(queries, block_index, 0, keepdims=False)
        own_block = (NKB - NQB + block_index).astype(jnp.int32)
        chosen_ids = lax.dynamic_index_in_dim(selected, block_index, 0, keepdims=False)
        part_list, max_list, sum_list = ([], [], [])
        for pick_slot in range(TOPK + 1):
            target = own_block if pick_slot == 0 else chosen_ids[pick_slot - 1].astype(jnp.int32)
            k_blk = lax.dynamic_index_in_dim(key_blocks, target, 0, keepdims=False)
            v_blk = lax.dynamic_index_in_dim(value_blocks, target, 0, keepdims=False)
            part_out, block_max, block_sum = partial_block(q_rows, k_blk, v_blk, positions, pick_slot == 0)
            part_list.append(part_out)
            max_list.append(block_max)
            sum_list.append(block_sum)
        stacked_parts = jnp.stack(part_list)
        stacked_max = jnp.stack(max_list)
        stacked_sum = jnp.stack(sum_list)
        best_max = lax.optimization_barrier(jnp.max(stacked_max, axis=0))
        scales = jnp.exp(stacked_max - best_max[None]) * stacked_sum
        shaped = stacked_parts.reshape(TOPK + 1, BLOCK, G * HQ, HD).astype(jnp.float32)
        summed = lax.optimization_barrier(jnp.sum(shaped * scales[..., None], axis=0))
        result = summed / lax.optimization_barrier(jnp.sum(scales, axis=0))[..., None]
        return result.reshape(BLOCK, G * HQ * HD).astype(jnp.bfloat16)
    return lax.map(one_query_block, jnp.arange(NQB, dtype=jnp.int32))
```

```python
import functools
import math

import jax
import jax.numpy as jnp
from jax import lax
from jax.experimental import pallas as pl
from jax.experimental.pallas import tpu as pltpu
from jax.sharding import Mesh, PartitionSpec as P

HD = 128
CTX = ("zp", "zl", "x", "y")
PAIR = ("zl", "x", "y", "c")


def exchange(value, axes):
    return lax.all_to_all(value, axes, split_axis=0, concat_axis=0, tiled=True)


def pick_kernel(index_ref, table_ref, out_ref):
    def body(step, carry):
        for inner in range(8):
            place = step * 8 + inner
            out_ref[place] = table_ref[index_ref[place]]
        return carry

    lax.fori_loop(0, out_ref.shape[0] // 8, body, 0)


def pick(index, table):
    count = index.shape[0]
    return pl.pallas_call(
        pick_kernel,
        out_shape=jax.ShapeDtypeStruct((count,) + table.shape[1:], table.dtype),
        in_specs=[
            pl.BlockSpec(memory_space=pltpu.SMEM),
            pl.BlockSpec(memory_space=pltpu.VMEM),
        ],
        out_specs=pl.BlockSpec(memory_space=pltpu.VMEM),
        name="pick",
    )(index, table)


def attend_kernel(own_keys, heads, q_ref, k_ref, v_ref, out_ref):
    rows = q_ref.shape[0]
    nt = (((1,), (1,)), ((), ()))
    scores = lax.dot_general(q_ref[...], k_ref[...], nt, preferred_element_type=jnp.float32)
    first = pl.program_id(0) * (rows // heads)
    token = first + lax.broadcasted_iota(jnp.int32, (rows, own_keys), 0) // heads
    key = lax.broadcasted_iota(jnp.int32, (rows, own_keys), 1)
    own = jnp.where(key_place(key, own_keys) <= token, scores[:, :own_keys], -jnp.inf)
    scores = jnp.concatenate([own, scores[:, own_keys:]], axis=1)
    best = jnp.max(scores, axis=1, keepdims=True)
    weights = jnp.exp((scores - best) * (1.0 / math.sqrt(HD))).astype(jnp.bfloat16)
    total = jnp.sum(weights.astype(jnp.float32), axis=1, keepdims=True)
    mixed = jnp.dot(weights, v_ref[...], preferred_element_type=jnp.float32)
    out_ref[...] = (mixed / total).astype(out_ref.dtype)


def key_place(key, own_keys):
    piece, inner = key // 8, key % 8
    return (piece % 2) * (own_keys // 2) + (piece // 2) * 8 + inner


def attend(q_rows, keys, values, own_keys, heads):
    rows, tile = q_rows.shape[0], 256
    whole = pl.BlockSpec(keys.shape, lambda i: (0, 0))
    part = pl.BlockSpec((tile, HD), lambda i: (i, 0))
    return pl.pallas_call(
        functools.partial(attend_kernel, own_keys, heads),
        grid=(rows // tile,),
        out_shape=jax.ShapeDtypeStruct(q_rows.shape, jnp.bfloat16),
        in_specs=[part, whole, whole],
        out_specs=part,
        name="attend",
    )(q_rows, keys, values)


def local(queries, key_blocks, value_blocks, selected):
    core = lax.axis_index("c")
    half_blocks, row_count, feat_width = queries.shape
    kv_count, block, kv_width = key_blocks.shape
    groups = kv_width // HD
    heads = feat_width // kv_width
    ctx_size = lax.axis_size(CTX)
    pair_size = lax.axis_size(PAIR)
    spots = ctx_size // groups
    piece = block // pair_size
    block_total = selected.shape[0]

    def spread(blocks):
        mine = lax.dynamic_slice_in_dim(blocks, core * (block // 2), block // 2, 1)
        mine = mine.reshape(kv_count, spots, piece, groups, HD)
        mine = mine.transpose(3, 1, 0, 2, 4).reshape(ctx_size, kv_count * piece, HD)
        return exchange(mine, CTX).reshape(ctx_size * kv_count, piece, HD)

    own_block = ctx_size * kv_count - block_total + jnp.arange(block_total, dtype=jnp.int32)
    targets = jnp.concatenate([own_block[:, None], selected], axis=1)
    width = targets.shape[1]
    index = targets.reshape(2, half_blocks, width).transpose(1, 0, 2).reshape(-1)

    def deliver(pieces):
        sent = pick(index, pieces).reshape(pair_size, width * piece, HD)
        got = exchange(sent, PAIR).reshape(pair_size, width, piece, HD)
        return got.transpose(1, 0, 2, 3).reshape(width * block, HD)

    keys = deliver(spread(key_blocks))
    values = deliver(spread(value_blocks))
    asked = queries.reshape(half_blocks, row_count, groups, heads, HD)
    asked = asked.transpose(2, 0, 1, 3, 4).reshape(ctx_size, row_count * heads, HD)
    asked = exchange(asked, CTX).reshape(-1, HD)
    done = attend(asked, keys, values, block, heads)
    back = exchange(done.reshape(ctx_size, row_count * heads, HD), CTX)
    back = back.reshape(groups, half_blocks, row_count, heads, HD)
    return back.transpose(1, 2, 0, 3, 4).reshape(queries.shape)


def solution(mesh):
    z_pairs = 4
    ctx_size, cores = mesh.devices.shape
    plane = 4
    fine = mesh.devices.reshape(z_pairs, ctx_size // (z_pairs * plane * plane), plane, plane, cores)
    fine_mesh = Mesh(fine, ("zp", "zl", "x", "y", "c"))
    in_specs = (P("c", CTX, None), P(CTX, None, None), P(CTX, None, None), P())
    out_specs = P("c", CTX, None)
    return jax.shard_map(
        local, mesh=fine_mesh, in_specs=in_specs, out_specs=out_specs, check_vma=False
    )
```

```python
import functools
import math

import jax
import jax.numpy as jnp
from jax import lax
from jax.experimental import pallas as pl
from jax.experimental.pallas import tpu as pltpu
from jax.sharding import Mesh, PartitionSpec as P

HD = 128
CTX = ("zp", "zl", "x", "y")
PAIR = ("zl", "x", "y", "c")


def exchange(value, axes):
    return lax.all_to_all(value, axes, split_axis=0, concat_axis=0, tiled=True)


def pick_kernel(index_ref, table_ref, out_ref):
    def body(step, carry):
        for inner in range(8):
            place = step * 8 + inner
            out_ref[place] = table_ref[index_ref[place]]
        return carry

    lax.fori_loop(0, out_ref.shape[0] // 8, body, 0)


def pick(index, table):
    count = index.shape[0]
    return pl.pallas_call(
        pick_kernel,
        out_shape=jax.ShapeDtypeStruct((count,) + table.shape[1:], table.dtype),
        in_specs=[
            pl.BlockSpec(memory_space=pltpu.SMEM),
            pl.BlockSpec(memory_space=pltpu.VMEM),
        ],
        out_specs=pl.BlockSpec(memory_space=pltpu.VMEM),
        name="pick",
    )(index, table)


def key_place(key, own_keys):
    piece, inner = key // 8, key % 8
    return (piece % 2) * (own_keys // 2) + (piece // 2) * 8 + inner


def attend_kernel(row_count, q_ref, kv_ref, out_ref, keys, values):
    sources, _, width, piece, _ = kv_ref.shape
    own_keys = sources * piece

    @pl.when(pl.program_id(0) == 0)
    def _():
        for j in range(width):
            place = pl.ds(j * own_keys, own_keys)
            keys[place] = kv_ref[:, 0, j].reshape(own_keys, HD)
            values[place] = kv_ref[:, 1, j].reshape(own_keys, HD)

    holders, rows_each, _ = q_ref.shape
    rows = holders * rows_each
    nt = (((1,), (1,)), ((), ()))
    asked = q_ref[...].reshape(rows, HD)
    scores = lax.dot_general(asked, keys[...], nt, preferred_element_type=jnp.float32)
    row = lax.broadcasted_iota(jnp.int32, (rows, 1), 0)
    token = (pl.program_id(0) * holders + row // rows_each) * row_count + row % row_count
    key = lax.broadcasted_iota(jnp.int32, (1, own_keys), 1)
    own = jnp.where(key_place(key, own_keys) <= token, scores[:, :own_keys], -jnp.inf)
    scores = jnp.concatenate([own, scores[:, own_keys:]], axis=1)
    best = jnp.max(scores, axis=1, keepdims=True)
    factor = math.log2(math.e) / math.sqrt(HD)
    weights = jnp.exp2((scores - best) * factor).astype(jnp.bfloat16)
    total = jnp.sum(weights.astype(jnp.float32), axis=1, keepdims=True)
    mixed = jnp.dot(weights, values[...], preferred_element_type=jnp.float32)
    out_ref[...] = (mixed / total).astype(out_ref.dtype).reshape(out_ref.shape)


def attend(arrived, pieces, row_count, rows_each):
    ctx_size, packed, _ = arrived.shape
    sources, _, width, piece, _ = pieces.shape
    holders = 16
    lead = packed // rows_each - 1
    return pl.pallas_call(
        functools.partial(attend_kernel, row_count),
        grid=(ctx_size // holders,),
        out_shape=jax.ShapeDtypeStruct((ctx_size, rows_each, HD), jnp.bfloat16),
        in_specs=[
            pl.BlockSpec((holders, rows_each, HD), lambda i: (i, lead, 0)),
            pl.BlockSpec(pieces.shape, lambda i: (0, 0, 0, 0, 0)),
        ],
        out_specs=pl.BlockSpec((holders, rows_each, HD), lambda i: (i, 0, 0)),
        scratch_shapes=[pltpu.VMEM((width * sources * piece, HD), jnp.bfloat16)] * 2,
        name="attend",
    )(arrived, pieces)


def local(queries, key_blocks, value_blocks, selected):
    core = lax.axis_index("c")
    half_blocks, row_count, feat_width = queries.shape
    kv_count, block, kv_width = key_blocks.shape
    groups = kv_width // HD
    heads = feat_width // kv_width
    ctx_size = lax.axis_size(CTX)
    pair_size = lax.axis_size(PAIR)
    spots = ctx_size // groups
    piece = block // pair_size

    def cut(blocks):
        mine = lax.dynamic_slice_in_dim(blocks, core * (block // 2), block // 2, 1)
        mine = mine.reshape(kv_count, spots, piece, groups, HD)
        return mine.transpose(3, 1, 0, 2, 4).reshape(ctx_size, kv_count * piece, HD)

    asked = queries.reshape(half_blocks, row_count, groups, heads, HD)
    asked = asked.transpose(2, 0, 3, 1, 4).reshape(ctx_size, heads * row_count, HD)
    parcels = jnp.concatenate([cut(key_blocks), cut(value_blocks), asked], axis=1)
    arrived = exchange(parcels, CTX)

    block_total = selected.shape[0]
    own_block = ctx_size * kv_count - block_total + jnp.arange(block_total, dtype=jnp.int32)
    targets = jnp.concatenate([own_block[:, None], selected], axis=1)
    width = targets.shape[1]
    targets = targets.reshape(2, half_blocks, 1, width).transpose(1, 0, 2, 3)
    in_parcel = parcels.shape[1] // piece
    place = targets // kv_count * in_parcel + targets % kv_count
    place = jnp.concatenate([place, place + kv_count], axis=2).reshape(-1)
    sent = pick(place, arrived.reshape(ctx_size * in_parcel, piece, HD))
    pieces = exchange(sent.reshape(pair_size, -1, HD), PAIR)
    pieces = pieces.reshape(pair_size, 2, width, piece, HD)
    done = attend(arrived, pieces, row_count, heads * row_count)
    back = exchange(done, CTX).reshape(groups, half_blocks, heads, row_count, HD)
    return back.transpose(1, 3, 0, 2, 4).reshape(queries.shape)


def solution(mesh):
    z_pairs = 4
    ctx_size, cores = mesh.devices.shape
    plane = 4
    fine = mesh.devices.reshape(z_pairs, ctx_size // (z_pairs * plane * plane), plane, plane, cores)
    fine_mesh = Mesh(fine, ("zp", "zl", "x", "y", "c"))
    in_specs = (P("c", CTX, None), P(CTX, None, None), P(CTX, None, None), P())
    out_specs = P("c", CTX, None)
    return jax.shard_map(
        local, mesh=fine_mesh, in_specs=in_specs, out_specs=out_specs, check_vma=False
    )
```

```python
import functools
import math

import jax
import jax.numpy as jnp
from jax import lax
from jax.experimental import pallas as pl
from jax.experimental.pallas import tpu as pltpu
from jax.sharding import Mesh, PartitionSpec as P

HD = 128
CTX = ("zp", "zl", "x", "y")
PAIR = ("zl", "x", "y", "c")


def exchange(value, axes):
    return lax.all_to_all(value, axes, split_axis=0, concat_axis=0, tiled=True)


def pack_kernel(core_ref, q_ref, k_ref, v_ref, out_ref):
    kv_count, _, _ = k_ref.shape
    spots, row_count, width = q_ref.shape
    piece = k_ref.shape[1] // spots
    at = 0
    for ref in (k_ref, v_ref):
        for block in range(kv_count):
            out_ref[:, at : at + piece] = ref[block].reshape(spots, piece, HD)
            at += piece
    for head in range(width // HD):
        out_ref[:, at : at + row_count] = q_ref[:, :, head * HD : (head + 1) * HD]
        at += row_count


def pack(core, queries, key_blocks, value_blocks):
    kv_count, block, kv_width = key_blocks.shape
    groups = kv_width // HD
    half_blocks, row_count, feat_width = queries.shape
    piece = block // 2 // half_blocks
    tall = 2 * kv_count * piece + feat_width // kv_width * row_count
    half = pl.BlockSpec((kv_count, block // 2, HD), lambda g, core_ref: (0, core_ref[0], g))
    return pl.pallas_call(
        pack_kernel,
        grid_spec=pltpu.PrefetchScalarGridSpec(
            num_scalar_prefetch=1,
            grid=(groups,),
            in_specs=[
                pl.BlockSpec(
                    (half_blocks, row_count, feat_width // groups),
                    lambda g, core_ref: (0, 0, g),
                ),
                half,
                half,
            ],
            out_specs=pl.BlockSpec((half_blocks, tall, HD), lambda g, core_ref: (g, 0, 0)),
        ),
        out_shape=jax.ShapeDtypeStruct((groups * half_blocks, tall, HD), queries.dtype),
        name="pack",
    )(core[None], queries, key_blocks, value_blocks)


def pick_kernel(index_ref, table_ref, out_ref):
    def body(step, carry):
        for inner in range(8):
            place = step * 8 + inner
            out_ref[place] = table_ref[index_ref[place]]
        return carry

    lax.fori_loop(0, out_ref.shape[0] // 8, body, 0)


def pick(index, table):
    count = index.shape[0]
    return pl.pallas_call(
        pick_kernel,
        out_shape=jax.ShapeDtypeStruct((count,) + table.shape[1:], table.dtype),
        in_specs=[
            pl.BlockSpec(memory_space=pltpu.SMEM),
            pl.BlockSpec(memory_space=pltpu.VMEM),
        ],
        out_specs=pl.BlockSpec(memory_space=pltpu.VMEM),
        name="pick",
    )(index, table)


def key_place(key, own_keys):
    piece, inner = key // 8, key % 8
    return (piece % 2) * (own_keys // 2) + (piece // 2) * 8 + inner


def attend_kernel(row_count, parts, q_ref, kv_ref, out_ref, keys, values):
    sources, _, width, piece, _ = kv_ref.shape
    own_keys = sources * piece
    holders, rows_each, _ = q_ref.shape
    holders = holders // parts
    rows = holders * rows_each
    factor = math.log2(math.e) / math.sqrt(HD)
    nt = (((1,), (1,)), ((), ()))

    @pl.when(pl.program_id(0) == 0)
    def _():
        for j in range(width):
            place = pl.ds(j * own_keys, own_keys)
            keys[place] = kv_ref[:, 0, j].reshape(own_keys, HD)
            values[place, :HD] = kv_ref[:, 1, j].reshape(own_keys, HD)
        values[:, HD:] = jnp.ones((width * own_keys, HD), jnp.bfloat16)

    def steps(part):
        held = pl.ds(part * holders, holders)
        asked = q_ref[held].reshape(rows, HD)
        scores = [
            lax.dot_general(
                asked,
                keys[pl.ds(j * own_keys, own_keys)],
                nt,
                preferred_element_type=jnp.float32,
            )
            for j in range(width)
        ]
        row = lax.broadcasted_iota(jnp.int32, (rows, 1), 0)
        holder = (pl.program_id(0) * parts + part) * holders + row // rows_each
        token = holder * row_count + row % row_count
        key = lax.broadcasted_iota(jnp.int32, (1, own_keys), 1)
        scores[0] = jnp.where(key_place(key, own_keys) <= token, scores[0], -jnp.inf)
        yield
        best = functools.reduce(jnp.maximum, scores)
        best = jnp.max(best, axis=1, keepdims=True)
        yield
        mixed = jnp.zeros((rows, 2 * HD), jnp.float32)
        for j in range(width):
            weights = jnp.exp2((scores[j] - best) * factor).astype(jnp.bfloat16)
            mixed += jnp.dot(
                weights,
                values[pl.ds(j * own_keys, own_keys)],
                preferred_element_type=jnp.float32,
            )
        result = mixed[:, :HD] / mixed[:, HD:]
        out_ref[held] = result.astype(out_ref.dtype).reshape(holders, rows_each, HD)
        yield

    running = [steps(part) for part in range(parts)]
    for _ in range(3):
        for one in running:
            next(one)


def attend(arrived, pieces, row_count, rows_each):
    ctx_size, packed, _ = arrived.shape
    sources, _, width, piece, _ = pieces.shape
    holders, parts = 64, 4
    lead = packed // rows_each - 1
    return pl.pallas_call(
        functools.partial(attend_kernel, row_count, parts),
        grid=(ctx_size // holders,),
        out_shape=jax.ShapeDtypeStruct((ctx_size, rows_each, HD), jnp.bfloat16),
        in_specs=[
            pl.BlockSpec((holders, rows_each, HD), lambda i: (i, lead, 0)),
            pl.BlockSpec(pieces.shape, lambda i: (0, 0, 0, 0, 0)),
        ],
        out_specs=pl.BlockSpec((holders, rows_each, HD), lambda i: (i, 0, 0)),
        scratch_shapes=[
            pltpu.VMEM((width * sources * piece, HD), jnp.bfloat16),
            pltpu.VMEM((width * sources * piece, 2 * HD), jnp.bfloat16),
        ],
        name="attend",
    )(arrived, pieces)


def local(queries, key_blocks, value_blocks, selected):
    core = lax.axis_index("c")
    half_blocks, row_count, feat_width = queries.shape
    kv_count, block, kv_width = key_blocks.shape
    groups = kv_width // HD
    heads = feat_width // kv_width
    ctx_size = lax.axis_size(CTX)
    pair_size = lax.axis_size(PAIR)
    piece = block // pair_size
    parcels = pack(core, queries, key_blocks, value_blocks)
    arrived = exchange(parcels, CTX)

    block_total = selected.shape[0]
    own_block = ctx_size * kv_count - block_total + jnp.arange(block_total, dtype=jnp.int32)
    targets = jnp.concatenate([own_block[:, None], selected], axis=1)
    width = targets.shape[1]
    targets = targets.reshape(2, half_blocks, 1, width).transpose(1, 0, 2, 3)
    in_parcel = parcels.shape[1] // piece
    place = targets // kv_count * in_parcel + targets % kv_count
    place = jnp.concatenate([place, place + kv_count], axis=2).reshape(-1)
    table = arrived.reshape(ctx_size * in_parcel, piece, HD)
    sent = pick(place, pltpu.with_memory_space_constraint(table, pltpu.VMEM))
    pieces = exchange(sent.reshape(pair_size, -1, HD), PAIR)
    pieces = pieces.reshape(pair_size, 2, width, piece, HD)
    done = attend(arrived, pieces, row_count, heads * row_count)
    back = exchange(done, CTX).reshape(groups, half_blocks, heads, row_count, HD)
    return back.transpose(1, 3, 0, 2, 4).reshape(queries.shape)


def solution(mesh):
    z_pairs = 4
    ctx_size, cores = mesh.devices.shape
    plane = 4
    fine = mesh.devices.reshape(z_pairs, ctx_size // (z_pairs * plane * plane), plane, plane, cores)
    fine_mesh = Mesh(fine, ("zp", "zl", "x", "y", "c"))
    in_specs = (P("c", CTX, None), P(CTX, None, None), P(CTX, None, None), P())
    out_specs = P("c", CTX, None)
    return jax.shard_map(
        local, mesh=fine_mesh, in_specs=in_specs, out_specs=out_specs, check_vma=False
    )
```

```python
import functools
import math

import jax
import jax.numpy as jnp
from jax import lax
from jax.experimental import pallas as pl
from jax.experimental.pallas import tpu as pltpu
from jax.sharding import Mesh, PartitionSpec as P

HD = 128
CTX = ("zp", "zl", "x", "y")
PAIR = ("zl", "x", "y", "c")


def exchange(value, axes):
    return lax.all_to_all(value, axes, split_axis=0, concat_axis=0, tiled=True)


def pack_kernel(core_ref, q_ref, k_ref, v_ref, out_ref, held, in_sems, out_sems):
    kv_count, spots, piece, kv_width = k_ref.shape
    _, row_count, feat_width = q_ref.shape
    groups = kv_width // HD
    heads = feat_width // kv_width

    def fetch(ref, g, one):
        return pltpu.make_async_copy(
            ref.at[one, :, :, pl.ds(g * HD, HD)],
            held.at[pl.ds(g * spots, spots), pl.ds(one * piece, piece)],
            in_sems.at[g, one],
        )

    def leave(g):
        part = pl.ds(g * spots, spots)
        return pltpu.make_async_copy(held.at[part], out_ref.at[part], out_sems.at[g])

    for core, ref in enumerate((k_ref, v_ref)):

        @pl.when(core_ref[0] == core)
        def _():
            for g in range(groups):
                for one in range(kv_count):
                    fetch(ref, g, one).start()

    for g in range(groups):
        for head in range(heads):
            rows = pl.ds(kv_count * piece + head * row_count, row_count)
            at = (g * heads + head) * HD
            held[pl.ds(g * spots, spots), rows] = q_ref[:, :, at : at + HD]
    for g in range(groups):
        for one in range(kv_count):
            fetch(k_ref, g, one).wait()
        leave(g).start()
    for g in range(groups):
        leave(g).wait()


def pack(core, queries, key_blocks, value_blocks):
    kv_count, block, kv_width = key_blocks.shape
    groups = kv_width // HD
    half_blocks, row_count, feat_width = queries.shape
    piece = block // half_blocks
    tall = kv_count * piece + feat_width // kv_width * row_count
    whole = jax.ShapeDtypeStruct((groups * half_blocks, tall, HD), queries.dtype)
    cut = (kv_count, half_blocks, piece, kv_width)
    away = pl.BlockSpec(memory_space=pl.ANY)
    return pl.pallas_call(
        pack_kernel,
        out_shape=whole,
        in_specs=[
            pl.BlockSpec(memory_space=pltpu.SMEM),
            pl.BlockSpec(memory_space=pltpu.VMEM),
            away,
            away,
        ],
        out_specs=away,
        scratch_shapes=[
            pltpu.VMEM(whole.shape, whole.dtype),
            pltpu.SemaphoreType.DMA((groups, kv_count)),
            pltpu.SemaphoreType.DMA((groups,)),
        ],
        name="pack",
    )(core[None], queries, key_blocks.reshape(cut), value_blocks.reshape(cut))


def pick_kernel(index_ref, table_ref, out_ref):
    def body(step, carry):
        for inner in range(8):
            place = step * 8 + inner
            out_ref[place] = table_ref[index_ref[place]]
        return carry

    lax.fori_loop(0, out_ref.shape[0] // 8, body, 0)


def pick(index, table):
    count = index.shape[0]
    return pl.pallas_call(
        pick_kernel,
        out_shape=jax.ShapeDtypeStruct((count,) + table.shape[1:], table.dtype),
        in_specs=[
            pl.BlockSpec(memory_space=pltpu.SMEM),
            pl.BlockSpec(memory_space=pltpu.VMEM),
        ],
        out_specs=pl.BlockSpec(memory_space=pltpu.VMEM),
        name="pick",
    )(index, table)


def attend_kernel(row_count, parts, q_ref, kv_ref, out_ref, keys, values):
    spots, _, width, piece, _ = kv_ref.shape
    own_keys = spots * piece
    ctx_size, rows_each, _ = q_ref.shape
    holders = ctx_size // parts
    rows = holders * rows_each
    factor = math.log2(math.e) / math.sqrt(HD)
    nt = (((1,), (1,)), ((), ()))
    for j in range(width):
        place = pl.ds(j * own_keys, own_keys)
        keys[place] = kv_ref[:, 0, j].reshape(own_keys, HD)
        values[place, :HD] = kv_ref[:, 1, j].reshape(own_keys, HD)
    values[:, HD:] = jnp.ones((width * own_keys, HD), jnp.bfloat16)

    def steps(part):
        held = pl.ds(part * holders, holders)
        asked = q_ref[held].reshape(rows, HD)
        seen = min(own_keys, -(-(part + 1) * holders * row_count // 128) * 128)
        spans = [(0, seen)] + [(j * own_keys, own_keys) for j in range(1, width)]
        scores = [
            lax.dot_general(asked, keys[pl.ds(*span)], nt, preferred_element_type=jnp.float32)
            for span in spans
        ]
        row = lax.broadcasted_iota(jnp.int32, (rows, 1), 0)
        token = (part * holders + row // rows_each) * row_count + row % row_count
        key = lax.broadcasted_iota(jnp.int32, (1, seen), 1)
        scores[0] = jnp.where(key <= token, scores[0], -jnp.inf)
        yield
        best = functools.reduce(jnp.maximum, [jnp.max(s, axis=1, keepdims=True) for s in scores])
        yield
        mixed = jnp.zeros((rows, 2 * HD), jnp.float32)
        for score, span in zip(scores, spans):
            weights = jnp.exp2((score - best) * factor).astype(jnp.bfloat16)
            mixed += jnp.dot(weights, values[pl.ds(*span)], preferred_element_type=jnp.float32)
        result = mixed[:, :HD] / mixed[:, HD:]
        out_ref[held] = result.astype(out_ref.dtype).reshape(holders, rows_each, HD)
        yield

    running = [steps(part) for part in range(parts)]
    for _ in range(3):
        for one in running:
            next(one)


def attend(arrived, pieces, row_count, rows_each):
    ctx_size, packed, _ = arrived.shape
    spots, _, width, piece, _ = pieces.shape
    parts = 8
    lead = packed // rows_each - 1
    return pl.pallas_call(
        functools.partial(attend_kernel, row_count, parts),
        grid=(1,),
        out_shape=jax.ShapeDtypeStruct((ctx_size, rows_each, HD), jnp.bfloat16),
        in_specs=[
            pl.BlockSpec((ctx_size, rows_each, HD), lambda i: (0, lead, 0)),
            pl.BlockSpec(pieces.shape, lambda i: (0, 0, 0, 0, 0)),
        ],
        out_specs=pl.BlockSpec((ctx_size, rows_each, HD), lambda i: (0, 0, 0)),
        scratch_shapes=[
            pltpu.VMEM((width * spots * piece, HD), jnp.bfloat16),
            pltpu.VMEM((width * spots * piece, 2 * HD), jnp.bfloat16),
        ],
        name="attend",
    )(arrived, pieces)


def local(queries, key_blocks, value_blocks, selected):
    core = lax.axis_index("c")
    half_blocks, row_count, feat_width = queries.shape
    kv_count, block, kv_width = key_blocks.shape
    groups = kv_width // HD
    heads = feat_width // kv_width
    ctx_size = lax.axis_size(CTX)
    pair_size = lax.axis_size(PAIR)
    piece = block // half_blocks
    parcels = pack(core, queries, key_blocks, value_blocks)
    arrived = exchange(parcels, CTX)

    block_total = selected.shape[0]
    own_block = ctx_size * kv_count - block_total + jnp.arange(block_total, dtype=jnp.int32)
    targets = jnp.concatenate([own_block[:, None], selected], axis=1)
    width = targets.shape[1]
    targets = targets.reshape(2, half_blocks, width).transpose(1, 0, 2).reshape(-1)
    in_parcel = parcels.shape[1] // piece
    place = targets // kv_count * in_parcel + targets % kv_count
    table = arrived.reshape(ctx_size * in_parcel, piece, HD)
    sent = pick(place, pltpu.with_memory_space_constraint(table, pltpu.VMEM))
    pieces = exchange(sent.reshape(pair_size, width * piece, HD), PAIR)
    pieces = pieces.reshape(half_blocks, 2, width, piece, HD)
    done = attend(arrived, pieces, row_count, heads * row_count)
    back = exchange(done, CTX).reshape(groups, half_blocks, heads, row_count, HD)
    return back.transpose(1, 3, 0, 2, 4).reshape(queries.shape)


def solution(mesh):
    z_pairs = 4
    ctx_size, cores = mesh.devices.shape
    plane = 4
    fine = mesh.devices.reshape(z_pairs, ctx_size // (z_pairs * plane * plane), plane, plane, cores)
    fine_mesh = Mesh(fine, ("zp", "zl", "x", "y", "c"))
    in_specs = (P("c", CTX, None), P(CTX, None, None), P(CTX, None, None), P())
    out_specs = P("c", CTX, None)
    return jax.shard_map(
        local, mesh=fine_mesh, in_specs=in_specs, out_specs=out_specs, check_vma=False
    )
```

```python
import functools
import math

import jax
import jax.numpy as jnp
from jax import lax
from jax.experimental import pallas as pl
from jax.experimental.pallas import tpu as pltpu
from jax.sharding import Mesh, PartitionSpec as P

HD = 128
CTX = ("zp", "zl", "x", "y")
PAIR = ("zl", "x", "y", "c")


def exchange(value, axes):
    return lax.all_to_all(value, axes, split_axis=0, concat_axis=0, tiled=True)


def pack_kernel(core_ref, q_ref, k_ref, v_ref, out_ref, asked, held, q_sem, in_sems, out_sems):
    kv_count, spots, piece, kv_width = k_ref.shape
    _, row_count, feat_width = q_ref.shape
    groups = kv_width // HD
    heads = feat_width // kv_width

    def fetch(ref, g, one):
        return pltpu.make_async_copy(
            ref.at[one, :, :, pl.ds(g * HD, HD)],
            held.at[pl.ds(g * spots, spots), pl.ds(one * piece, piece)],
            in_sems.at[g, one],
        )

    def leave(g):
        part = pl.ds(g * spots, spots)
        return pltpu.make_async_copy(held.at[part], out_ref.at[part], out_sems.at[g])

    whole = pltpu.make_async_copy(q_ref, asked, q_sem)
    whole.start()
    for core, ref in enumerate((k_ref, v_ref)):

        @pl.when(core_ref[0] == core)
        def _():
            for g in range(groups):
                for one in range(kv_count):
                    fetch(ref, g, one).start()

    whole.wait()
    for g in range(groups):
        for head in range(heads):
            rows = pl.ds(kv_count * piece + head * row_count, row_count)
            at = (g * heads + head) * HD
            held[pl.ds(g * spots, spots), rows] = asked[:, :, at : at + HD]
    for g in range(groups):
        for one in range(kv_count):
            fetch(k_ref, g, one).wait()
        leave(g).start()
    for g in range(groups):
        leave(g).wait()


def pack(core, queries, key_blocks, value_blocks):
    kv_count, block, kv_width = key_blocks.shape
    groups = kv_width // HD
    half_blocks, row_count, feat_width = queries.shape
    piece = block // half_blocks
    tall = kv_count * piece + feat_width // kv_width * row_count
    whole = jax.ShapeDtypeStruct((groups * half_blocks, tall, HD), queries.dtype)
    cut = (kv_count, half_blocks, piece, kv_width)
    away = pl.BlockSpec(memory_space=pl.ANY)
    return pl.pallas_call(
        pack_kernel,
        out_shape=whole,
        in_specs=[
            pl.BlockSpec(memory_space=pltpu.SMEM),
            away,
            away,
            away,
        ],
        out_specs=away,
        scratch_shapes=[
            pltpu.VMEM(queries.shape, queries.dtype),
            pltpu.VMEM(whole.shape, whole.dtype),
            pltpu.SemaphoreType.DMA(()),
            pltpu.SemaphoreType.DMA((groups, kv_count)),
            pltpu.SemaphoreType.DMA((groups,)),
        ],
        name="pack",
    )(core[None], queries, key_blocks.reshape(cut), value_blocks.reshape(cut))


def pick_kernel(index_ref, table_ref, out_ref):
    def body(step, carry):
        for inner in range(8):
            place = step * 8 + inner
            out_ref[place] = table_ref[index_ref[place]]
        return carry

    lax.fori_loop(0, out_ref.shape[0] // 8, body, 0)


def pick(index, table):
    count = index.shape[0]
    return pl.pallas_call(
        pick_kernel,
        out_shape=jax.ShapeDtypeStruct((count,) + table.shape[1:], table.dtype),
        in_specs=[
            pl.BlockSpec(memory_space=pltpu.SMEM),
            pl.BlockSpec(memory_space=pltpu.VMEM),
        ],
        out_specs=pl.BlockSpec(memory_space=pltpu.VMEM),
        name="pick",
    )(index, table)


def attend_kernel(row_count, parts, q_ref, kv_ref, out_ref, keys, values, ready, sems):
    spots, _, width, piece, _ = kv_ref.shape
    own_keys = spots * piece
    ctx_size, rows_each, _ = out_ref.shape
    lead = q_ref.shape[1] - rows_each
    holders = ctx_size // parts
    rows = holders * rows_each
    factor = math.log2(math.e) / math.sqrt(HD)
    nt = (((1,), (1,)), ((), ()))
    for j in range(width):
        place = pl.ds(j * own_keys, own_keys)
        keys[place] = kv_ref[:, 0, j].reshape(own_keys, HD)
        values[place, :HD] = kv_ref[:, 1, j].reshape(own_keys, HD)
    values[:, HD:] = jnp.ones((width * own_keys, HD), jnp.bfloat16)

    def steps(part):
        held = pl.ds(part * holders, holders)
        asked = q_ref[held, lead:].reshape(rows, HD)
        seen = min(own_keys, -(-(part + 1) * holders * row_count // 128) * 128)
        spans = [(0, seen)] + [(j * own_keys, own_keys) for j in range(1, width)]
        scores = [
            lax.dot_general(asked, keys[pl.ds(*span)], nt, preferred_element_type=jnp.float32)
            for span in spans
        ]
        row = lax.broadcasted_iota(jnp.int32, (rows, 1), 0)
        token = (part * holders + row // rows_each) * row_count + row % row_count
        key = lax.broadcasted_iota(jnp.int32, (1, seen), 1)
        scores[0] = jnp.where(key <= token, scores[0], -jnp.inf)
        yield
        best = functools.reduce(jnp.maximum, [jnp.max(s, axis=1, keepdims=True) for s in scores])
        yield
        mixed = jnp.zeros((rows, 2 * HD), jnp.float32)
        for score, span in zip(scores, spans):
            weights = jnp.exp2((score - best) * factor).astype(jnp.bfloat16)
            mixed += jnp.dot(weights, values[pl.ds(*span)], preferred_element_type=jnp.float32)
        result = mixed[:, :HD] / mixed[:, HD:]
        ready[held] = result.astype(out_ref.dtype).reshape(holders, rows_each, HD)
        leave(part).start()
        yield

    def leave(part):
        held = pl.ds(part * holders, holders)
        return pltpu.make_async_copy(ready.at[held], out_ref.at[held], sems.at[part])

    running = [steps(part) for part in range(parts)]
    for _ in range(3):
        for one in running:
            next(one)
    for part in range(parts):
        leave(part).wait()


def attend(arrived, pieces, row_count, rows_each):
    ctx_size = arrived.shape[0]
    spots, _, width, piece, _ = pieces.shape
    parts = 8
    whole = jax.ShapeDtypeStruct((ctx_size, rows_each, HD), jnp.bfloat16)
    near = pl.BlockSpec(memory_space=pltpu.VMEM)
    return pl.pallas_call(
        functools.partial(attend_kernel, row_count, parts),
        out_shape=whole,
        in_specs=[near, near],
        out_specs=pl.BlockSpec(memory_space=pl.ANY),
        scratch_shapes=[
            pltpu.VMEM((width * spots * piece, HD), jnp.bfloat16),
            pltpu.VMEM((width * spots * piece, 2 * HD), jnp.bfloat16),
            pltpu.VMEM(whole.shape, whole.dtype),
            pltpu.SemaphoreType.DMA((parts,)),
        ],
        compiler_params=pltpu.CompilerParams(vmem_limit_bytes=48 * 2**20),
        name="attend",
    )(
        pltpu.with_memory_space_constraint(arrived, pltpu.VMEM),
        pltpu.with_memory_space_constraint(pieces, pltpu.VMEM),
    )


def unpack_kernel(back_ref, out_ref):
    spots, row_count, feat_width = out_ref.shape
    heads = back_ref.shape[1] // row_count
    for g in range(back_ref.shape[0] // spots):
        for head in range(heads):
            at = (g * heads + head) * HD
            rows = pl.ds(head * row_count, row_count)
            out_ref[:, :, at : at + HD] = back_ref[g * spots : (g + 1) * spots, rows]


def unpack(back, shape):
    near = pl.BlockSpec(memory_space=pltpu.VMEM)
    return pl.pallas_call(
        unpack_kernel,
        out_shape=jax.ShapeDtypeStruct(shape, back.dtype),
        in_specs=[near],
        out_specs=near,
        name="unpack",
    )(pltpu.with_memory_space_constraint(back, pltpu.VMEM))


def local(queries, key_blocks, value_blocks, selected):
    core = lax.axis_index("c")
    half_blocks, row_count, feat_width = queries.shape
    kv_count, block, kv_width = key_blocks.shape
    groups = kv_width // HD
    heads = feat_width // kv_width
    ctx_size = lax.axis_size(CTX)
    pair_size = lax.axis_size(PAIR)
    piece = block // half_blocks
    parcels = pack(core, queries, key_blocks, value_blocks)
    arrived = exchange(parcels, CTX)

    block_total = selected.shape[0]
    own_block = ctx_size * kv_count - block_total + jnp.arange(block_total, dtype=jnp.int32)
    targets = jnp.concatenate([own_block[:, None], selected], axis=1)
    width = targets.shape[1]
    targets = targets.reshape(2, half_blocks, width).transpose(1, 0, 2).reshape(-1)
    in_parcel = parcels.shape[1] // piece
    place = targets // kv_count * in_parcel + targets % kv_count
    table = arrived.reshape(ctx_size * in_parcel, piece, HD)
    sent = pick(place, pltpu.with_memory_space_constraint(table, pltpu.VMEM))
    pieces = exchange(sent.reshape(pair_size, width * piece, HD), PAIR)
    pieces = pieces.reshape(half_blocks, 2, width, piece, HD)
    done = attend(arrived, pieces, row_count, heads * row_count)
    return unpack(exchange(done, CTX), queries.shape)


def solution(mesh):
    z_pairs = 4
    ctx_size, cores = mesh.devices.shape
    plane = 4
    fine = mesh.devices.reshape(z_pairs, ctx_size // (z_pairs * plane * plane), plane, plane, cores)
    fine_mesh = Mesh(fine, ("zp", "zl", "x", "y", "c"))
    in_specs = (P("c", CTX, None), P(CTX, None, None), P(CTX, None, None), P())
    out_specs = P("c", CTX, None)
    return jax.shard_map(
        local, mesh=fine_mesh, in_specs=in_specs, out_specs=out_specs, check_vma=False
    )
```

```python
import functools
import math

import jax
import jax.numpy as jnp
from jax import lax
from jax.experimental import pallas as pl
from jax.experimental.pallas import tpu as pltpu
from jax.sharding import Mesh, PartitionSpec as P

HD = 128
CTX = ("zp", "zl", "x", "y")
PAIR = ("zl", "x", "y", "c")


def exchange(value, axes):
    return lax.all_to_all(value, axes, split_axis=0, concat_axis=0, tiled=True)


def pack_kernel(core_ref, q_ref, k_ref, v_ref, out_ref, asked, held, q_sem, in_sems, out_sems):
    kv_count, spots, piece, kv_width = k_ref.shape
    _, row_count, feat_width = q_ref.shape
    groups = kv_width // HD
    heads = feat_width // kv_width

    def fetch(ref, g, one):
        return pltpu.make_async_copy(
            ref.at[one, :, :, pl.ds(g * HD, HD)],
            held.at[pl.ds(g * spots, spots), pl.ds(one * piece, piece)],
            in_sems.at[g, one],
        )

    def leave(g):
        part = pl.ds(g * spots, spots)
        return pltpu.make_async_copy(held.at[part], out_ref.at[part], out_sems.at[g])

    whole = pltpu.make_async_copy(q_ref, asked, q_sem)
    whole.start()
    for core, ref in enumerate((k_ref, v_ref)):

        @pl.when(core_ref[0] == core)
        def _():
            for g in range(groups):
                for one in range(kv_count):
                    fetch(ref, g, one).start()

    whole.wait()
    for g in range(groups):
        for head in range(heads):
            rows = pl.ds(kv_count * piece + head * row_count, row_count)
            at = (g * heads + head) * HD
            held[pl.ds(g * spots, spots), rows] = asked[:, :, at : at + HD]
    for g in range(groups):
        for one in range(kv_count):
            fetch(k_ref, g, one).wait()
        leave(g).start()
    for g in range(groups):
        leave(g).wait()


def pack(core, queries, key_blocks, value_blocks):
    kv_count, block, kv_width = key_blocks.shape
    groups = kv_width // HD
    half_blocks, row_count, feat_width = queries.shape
    piece = block // half_blocks
    tall = kv_count * piece + feat_width // kv_width * row_count
    whole = jax.ShapeDtypeStruct((groups * half_blocks, tall, HD), queries.dtype)
    cut = (kv_count, half_blocks, piece, kv_width)
    away = pl.BlockSpec(memory_space=pl.ANY)
    return pl.pallas_call(
        pack_kernel,
        out_shape=whole,
        in_specs=[
            pl.BlockSpec(memory_space=pltpu.SMEM),
            away,
            away,
            away,
        ],
        out_specs=away,
        scratch_shapes=[
            pltpu.VMEM(queries.shape, queries.dtype),
            pltpu.VMEM(whole.shape, whole.dtype),
            pltpu.SemaphoreType.DMA(()),
            pltpu.SemaphoreType.DMA((groups, kv_count)),
            pltpu.SemaphoreType.DMA((groups,)),
        ],
        name="pack",
    )(core[None], queries, key_blocks.reshape(cut), value_blocks.reshape(cut))


def pick_kernel(index_ref, table_ref, out_ref):
    def body(step, carry):
        for inner in range(8):
            place = step * 8 + inner
            out_ref[place] = table_ref[index_ref[place]]
        return carry

    lax.fori_loop(0, out_ref.shape[0] // 8, body, 0)


def pick(index, table):
    count = index.shape[0]
    return pl.pallas_call(
        pick_kernel,
        out_shape=jax.ShapeDtypeStruct((count,) + table.shape[1:], table.dtype),
        in_specs=[
            pl.BlockSpec(memory_space=pltpu.SMEM),
            pl.BlockSpec(memory_space=pltpu.VMEM),
        ],
        out_specs=pl.BlockSpec(memory_space=pltpu.VMEM),
        compiler_params=pltpu.CompilerParams(vmem_limit_bytes=32 * 2**20),
        name="pick",
    )(index, table)


def attend_kernel(row_count, parts, q_ref, kv_ref, out_ref, keys, values):
    spots, _, width, piece, _ = kv_ref.shape
    own_keys = spots * piece
    ctx_size, rows_each, _ = out_ref.shape
    lead = q_ref.shape[1] - rows_each
    holders = ctx_size // parts
    rows = holders * rows_each
    factor = math.log2(math.e) / math.sqrt(HD)
    nt = (((1,), (1,)), ((), ()))
    for j in range(width):
        place = pl.ds(j * own_keys, own_keys)
        keys[place] = kv_ref[:, 0, j].reshape(own_keys, HD)
        values[place, :HD] = kv_ref[:, 1, j].reshape(own_keys, HD)
    values[:, HD:] = jnp.ones((width * own_keys, HD), jnp.bfloat16)

    def steps(part):
        held = pl.ds(part * holders, holders)
        asked = q_ref[held, lead:].reshape(rows, HD)
        seen = min(own_keys, -(-(part + 1) * holders * row_count // 128) * 128)
        spans = [(0, seen)] + [(j * own_keys, own_keys) for j in range(1, width)]
        scores = [
            lax.dot_general(asked, keys[pl.ds(*span)], nt, preferred_element_type=jnp.float32)
            for span in spans
        ]
        row = lax.broadcasted_iota(jnp.int32, (rows, 1), 0)
        token = (part * holders + row // rows_each) * row_count + row % row_count
        key = lax.broadcasted_iota(jnp.int32, (1, seen), 1)
        scores[0] = jnp.where(key <= token, scores[0], -jnp.inf)
        yield
        best = functools.reduce(jnp.maximum, [jnp.max(s, axis=1, keepdims=True) for s in scores])
        yield
        mixed = jnp.zeros((rows, 2 * HD), jnp.float32)
        for score, span in zip(scores, spans):
            weights = jnp.exp2((score - best) * factor).astype(jnp.bfloat16)
            mixed += jnp.dot(weights, values[pl.ds(*span)], preferred_element_type=jnp.float32)
        result = mixed[:, :HD] / mixed[:, HD:]
        out_ref[held] = result.astype(out_ref.dtype).reshape(holders, rows_each, HD)
        yield

    running = [steps(part) for part in range(parts)]
    for _ in range(3):
        for one in running:
            next(one)


def attend(arrived, pieces, row_count, rows_each):
    ctx_size = arrived.shape[0]
    spots, _, width, piece, _ = pieces.shape
    parts = 8
    whole = jax.ShapeDtypeStruct((ctx_size, rows_each, HD), jnp.bfloat16)
    near = pl.BlockSpec(memory_space=pltpu.VMEM)
    return pl.pallas_call(
        functools.partial(attend_kernel, row_count, parts),
        out_shape=whole,
        in_specs=[near, near],
        out_specs=near,
        scratch_shapes=[
            pltpu.VMEM((width * spots * piece, HD), jnp.bfloat16),
            pltpu.VMEM((width * spots * piece, 2 * HD), jnp.bfloat16),
        ],
        compiler_params=pltpu.CompilerParams(vmem_limit_bytes=48 * 2**20),
        name="attend",
    )(
        pltpu.with_memory_space_constraint(arrived, pltpu.VMEM),
        pltpu.with_memory_space_constraint(pieces, pltpu.VMEM),
    )


def unpack_kernel(back_ref, out_ref):
    spots, row_count, feat_width = out_ref.shape
    heads = back_ref.shape[1] // row_count
    for g in range(back_ref.shape[0] // spots):
        for head in range(heads):
            at = (g * heads + head) * HD
            rows = pl.ds(head * row_count, row_count)
            out_ref[:, :, at : at + HD] = back_ref[g * spots : (g + 1) * spots, rows]


def unpack(back, shape):
    near = pl.BlockSpec(memory_space=pltpu.VMEM)
    return pl.pallas_call(
        unpack_kernel,
        out_shape=jax.ShapeDtypeStruct(shape, back.dtype),
        in_specs=[near],
        out_specs=near,
        name="unpack",
    )(pltpu.with_memory_space_constraint(back, pltpu.VMEM))


def local(queries, key_blocks, value_blocks, selected):
    core = lax.axis_index("c")
    half_blocks, row_count, feat_width = queries.shape
    kv_count, block, kv_width = key_blocks.shape
    groups = kv_width // HD
    heads = feat_width // kv_width
    ctx_size = lax.axis_size(CTX)
    pair_size = lax.axis_size(PAIR)
    piece = block // half_blocks
    parcels = pack(core, queries, key_blocks, value_blocks)
    arrived = exchange(parcels, CTX)

    block_total = selected.shape[0]
    own_block = ctx_size * kv_count - block_total + jnp.arange(block_total, dtype=jnp.int32)
    targets = jnp.concatenate([own_block[:, None], selected], axis=1)
    width = targets.shape[1]
    targets = targets.reshape(2, half_blocks, width).transpose(1, 0, 2).reshape(-1)
    in_parcel = parcels.shape[1] // piece
    place = targets // kv_count * in_parcel + targets % kv_count
    table = arrived.reshape(ctx_size * in_parcel, piece, HD)
    sent = pick(place, pltpu.with_memory_space_constraint(table, pltpu.VMEM))
    pieces = exchange(sent.reshape(pair_size, width * piece, HD), PAIR)
    pieces = pieces.reshape(half_blocks, 2, width, piece, HD)
    done = attend(arrived, pieces, row_count, heads * row_count)
    return unpack(exchange(done, CTX), queries.shape)


def solution(mesh):
    z_pairs = 4
    ctx_size, cores = mesh.devices.shape
    plane = 4
    fine = mesh.devices.reshape(z_pairs, ctx_size // (z_pairs * plane * plane), plane, plane, cores)
    fine_mesh = Mesh(fine, ("zp", "zl", "x", "y", "c"))
    in_specs = (P("c", CTX, None), P(CTX, None, None), P(CTX, None, None), P())
    out_specs = P("c", CTX, None)
    return jax.shard_map(
        local, mesh=fine_mesh, in_specs=in_specs, out_specs=out_specs, check_vma=False
    )
```

```python
import functools
import math

import jax
import jax.numpy as jnp
from jax import lax
from jax.experimental import pallas as pl
from jax.experimental.pallas import tpu as pltpu
from jax.sharding import Mesh, PartitionSpec as P

HD = 128
CTX = ("zp", "zl", "x", "y")
PAIR = ("zl", "x", "y", "c")


def exchange(value, axes):
    return lax.all_to_all(value, axes, split_axis=0, concat_axis=0, tiled=True)


def pack_kernel(
    core_ref, chosen_ref, q_ref, k_ref, v_ref, out_ref, place_ref, asked, q_sem, in_sems
):
    kv_count, spots, piece, kv_width = k_ref.shape
    _, row_count, feat_width = q_ref.shape
    groups = kv_width // HD
    heads = feat_width // kv_width

    def fetch(ref, g, one):
        return pltpu.make_async_copy(
            ref.at[one, :, :, pl.ds(g * HD, HD)],
            out_ref.at[pl.ds(g * spots, spots), pl.ds(one * piece, piece)],
            in_sems.at[g, one],
        )

    whole = pltpu.make_async_copy(q_ref, asked, q_sem)
    whole.start()
    for core, ref in enumerate((k_ref, v_ref)):

        @pl.when(core_ref[0] == core)
        def _():
            for g in range(groups):
                for one in range(kv_count):
                    fetch(ref, g, one).start()

    topk, block_total = chosen_ref.shape
    width = topk + 1
    in_parcel = out_ref.shape[1] // piece
    first_own = out_ref.shape[0] * kv_count - block_total

    def note(spot, carry):
        for half in range(2):
            asker = half * spots + spot
            named = [first_own + asker] + [chosen_ref[j, asker] for j in range(topk)]
            for j, target in enumerate(named):
                holder = lax.div(target, kv_count)
                inner = target - holder * kv_count
                place_ref[(spot * 2 + half) * width + j] = holder * in_parcel + inner
        return carry

    lax.fori_loop(0, spots, note, 0)
    whole.wait()
    for g in range(groups):
        for head in range(heads):
            rows = pl.ds(kv_count * piece + head * row_count, row_count)
            at = (g * heads + head) * HD
            out_ref[pl.ds(g * spots, spots), rows] = asked[:, :, at : at + HD]
    for g in range(groups):
        for one in range(kv_count):
            fetch(k_ref, g, one).wait()


def pack(core, selected, queries, key_blocks, value_blocks):
    kv_count, block, kv_width = key_blocks.shape
    groups = kv_width // HD
    half_blocks, row_count, feat_width = queries.shape
    piece = block // half_blocks
    tall = kv_count * piece + feat_width // kv_width * row_count
    cut = (kv_count, half_blocks, piece, kv_width)
    scalars = pl.BlockSpec(memory_space=pltpu.SMEM)
    away = pl.BlockSpec(memory_space=pltpu.HBM)
    count = selected.shape[0] * (selected.shape[1] + 1)
    return pl.pallas_call(
        pack_kernel,
        out_shape=(
            jax.ShapeDtypeStruct((groups * half_blocks, tall, HD), queries.dtype),
            jax.ShapeDtypeStruct((count,), jnp.int32),
        ),
        in_specs=[scalars, scalars, away, away, away],
        out_specs=(pl.BlockSpec(memory_space=pltpu.VMEM), scalars),
        scratch_shapes=[
            pltpu.VMEM(queries.shape, queries.dtype),
            pltpu.SemaphoreType.DMA(()),
            pltpu.SemaphoreType.DMA((groups, kv_count)),
        ],
        compiler_params=pltpu.CompilerParams(vmem_limit_bytes=32 * 2**20),
        name="pack",
    )(
        core[None],
        *(
            pltpu.with_memory_space_constraint(array, pltpu.HBM)
            for array in (selected.T, queries, key_blocks.reshape(cut), value_blocks.reshape(cut))
        ),
    )


def pick_kernel(index_ref, table_ref, out_ref):
    def body(step, carry):
        for inner in range(8):
            place = step * 8 + inner
            out_ref[place] = table_ref[index_ref[place]]
        return carry

    lax.fori_loop(0, out_ref.shape[0] // 8, body, 0)


def pick(index, table):
    count = index.shape[0]
    return pl.pallas_call(
        pick_kernel,
        out_shape=jax.ShapeDtypeStruct((count,) + table.shape[1:], table.dtype),
        in_specs=[
            pl.BlockSpec(memory_space=pltpu.SMEM),
            pl.BlockSpec(memory_space=pltpu.VMEM),
        ],
        out_specs=pl.BlockSpec(memory_space=pltpu.VMEM),
        compiler_params=pltpu.CompilerParams(vmem_limit_bytes=32 * 2**20),
        name="pick",
    )(index, table)


def attend_kernel(row_count, parts, q_ref, kv_ref, out_ref, keys, values):
    spots, _, width, piece, _ = kv_ref.shape
    own_keys = spots * piece
    ctx_size, rows_each, _ = out_ref.shape
    lead = q_ref.shape[1] - rows_each
    holders = ctx_size // parts
    rows = holders * rows_each
    factor = math.log2(math.e) / math.sqrt(HD)
    nt = (((1,), (1,)), ((), ()))
    for j in range(width):
        place = pl.ds(j * own_keys, own_keys)
        keys[place] = kv_ref[:, 0, j].reshape(own_keys, HD)
        values[place, :HD] = kv_ref[:, 1, j].reshape(own_keys, HD)
    values[:, HD:] = jnp.ones((width * own_keys, HD), jnp.bfloat16)

    def steps(part):
        held = pl.ds(part * holders, holders)
        asked = q_ref[held, lead:].reshape(rows, HD)
        seen = min(own_keys, -(-(part + 1) * holders * row_count // 128) * 128)
        spans = [(0, seen)] + [(j * own_keys, own_keys) for j in range(1, width)]
        scores = [
            lax.dot_general(asked, keys[pl.ds(*span)], nt, preferred_element_type=jnp.float32)
            for span in spans
        ]
        row = lax.broadcasted_iota(jnp.int32, (rows, 1), 0)
        token = (part * holders + row // rows_each) * row_count + row % row_count
        key = lax.broadcasted_iota(jnp.int32, (1, seen), 1)
        scores[0] = jnp.where(key <= token, scores[0], -jnp.inf)
        yield
        best = functools.reduce(jnp.maximum, [jnp.max(s, axis=1, keepdims=True) for s in scores])
        yield
        mixed = jnp.zeros((rows, 2 * HD), jnp.float32)
        for score, span in zip(scores, spans):
            weights = jnp.exp2((score - best) * factor).astype(jnp.bfloat16)
            mixed += jnp.dot(weights, values[pl.ds(*span)], preferred_element_type=jnp.float32)
        result = mixed[:, :HD] / mixed[:, HD:]
        out_ref[held] = result.astype(out_ref.dtype).reshape(holders, rows_each, HD)
        yield

    running = [steps(part) for part in range(parts)]
    for _ in range(3):
        for one in running:
            next(one)


def attend(arrived, pieces, row_count, rows_each):
    ctx_size = arrived.shape[0]
    spots, _, width, piece, _ = pieces.shape
    parts = 8
    whole = jax.ShapeDtypeStruct((ctx_size, rows_each, HD), jnp.bfloat16)
    near = pl.BlockSpec(memory_space=pltpu.VMEM)
    return pl.pallas_call(
        functools.partial(attend_kernel, row_count, parts),
        out_shape=whole,
        in_specs=[near, near],
        out_specs=near,
        scratch_shapes=[
            pltpu.VMEM((width * spots * piece, HD), jnp.bfloat16),
            pltpu.VMEM((width * spots * piece, 2 * HD), jnp.bfloat16),
        ],
        compiler_params=pltpu.CompilerParams(vmem_limit_bytes=48 * 2**20),
        name="attend",
    )(
        pltpu.with_memory_space_constraint(arrived, pltpu.VMEM),
        pltpu.with_memory_space_constraint(pieces, pltpu.VMEM),
    )


def unpack_kernel(back_ref, out_ref):
    spots, row_count, feat_width = out_ref.shape
    heads = back_ref.shape[1] // row_count
    for g in range(back_ref.shape[0] // spots):
        for head in range(heads):
            at = (g * heads + head) * HD
            rows = pl.ds(head * row_count, row_count)
            out_ref[:, :, at : at + HD] = back_ref[g * spots : (g + 1) * spots, rows]


def unpack(back, shape):
    near = pl.BlockSpec(memory_space=pltpu.VMEM)
    return pl.pallas_call(
        unpack_kernel,
        out_shape=jax.ShapeDtypeStruct(shape, back.dtype),
        in_specs=[near],
        out_specs=near,
        name="unpack",
    )(pltpu.with_memory_space_constraint(back, pltpu.VMEM))


def local(queries, key_blocks, value_blocks, selected):
    core = lax.axis_index("c")
    half_blocks, row_count, feat_width = queries.shape
    kv_count, block, kv_width = key_blocks.shape
    groups = kv_width // HD
    heads = feat_width // kv_width
    ctx_size = lax.axis_size(CTX)
    pair_size = lax.axis_size(PAIR)
    piece = block // half_blocks
    width = selected.shape[1] + 1
    parcels, place = pack(core, selected, queries, key_blocks, value_blocks)
    arrived = exchange(parcels, CTX)
    table = arrived.reshape(-1, piece, HD)
    sent = pick(place, pltpu.with_memory_space_constraint(table, pltpu.VMEM))
    pieces = exchange(sent.reshape(pair_size, width * piece, HD), PAIR)
    pieces = pieces.reshape(half_blocks, 2, width, piece, HD)
    done = attend(arrived, pieces, row_count, heads * row_count)
    return unpack(exchange(done, CTX), queries.shape)


def solution(mesh):
    z_pairs = 4
    ctx_size, cores = mesh.devices.shape
    plane = 4
    fine = mesh.devices.reshape(z_pairs, ctx_size // (z_pairs * plane * plane), plane, plane, cores)
    fine_mesh = Mesh(fine, ("zp", "zl", "x", "y", "c"))
    in_specs = (P("c", CTX, None), P(CTX, None, None), P(CTX, None, None), P())
    out_specs = P("c", CTX, None)
    return jax.shard_map(
        local, mesh=fine_mesh, in_specs=in_specs, out_specs=out_specs, check_vma=False
    )
```

```python
import functools
import math

import jax
import jax.numpy as jnp
from jax import lax
from jax.experimental import pallas as pl
from jax.experimental.pallas import tpu as pltpu
from jax.sharding import Mesh, PartitionSpec as P

HD = 128
CTX = ("zp", "zl", "x", "y")
SPREAD = ("zl", "x", "y", "zp")
PAIR = ("zl", "x", "y", "c")


def exchange(value, axes):
    return lax.all_to_all(value, axes, split_axis=0, concat_axis=0, tiled=True)


def pack_kernel(
    core_ref, chosen_ref, q_ref, k_ref, v_ref, out_ref, place_ref, asked, q_sem, in_sems
):
    kv_count, spots, piece, kv_width = k_ref.shape
    _, row_count, feat_width = q_ref.shape
    groups = kv_width // HD
    heads = feat_width // kv_width

    def fetch(ref, g, one):
        return pltpu.make_async_copy(
            ref.at[one, :, :, pl.ds(g * HD, HD)],
            out_ref.at[:, g, pl.ds(one * piece, piece)],
            in_sems.at[g, one],
        )

    whole = pltpu.make_async_copy(q_ref, asked, q_sem)
    whole.start()
    for core, ref in enumerate((k_ref, v_ref)):

        @pl.when(core_ref[0] == core)
        def _():
            for g in range(groups):
                for one in range(kv_count):
                    fetch(ref, g, one).start()

    topk, block_total = chosen_ref.shape
    width = topk + 1
    in_parcel = out_ref.shape[2] // piece
    first_own = spots * groups * kv_count - block_total

    def note(spot, carry):
        for half in range(2):
            asker = half * spots + spot
            named = [first_own + asker] + [chosen_ref[j, asker] for j in range(topk)]
            for j, target in enumerate(named):
                holder = lax.div(target, kv_count)
                inner = target - holder * kv_count
                pair = lax.div(holder, spots)
                came = (holder - pair * spots) * groups + pair
                place_ref[(spot * 2 + half) * width + j] = came * in_parcel + inner
        return carry

    lax.fori_loop(0, spots, note, 0)
    whole.wait()
    for g in range(groups):
        for head in range(heads):
            rows = pl.ds(kv_count * piece + head * row_count, row_count)
            at = (g * heads + head) * HD
            out_ref[:, g, rows] = asked[:, :, at : at + HD]
    for g in range(groups):
        for one in range(kv_count):
            fetch(k_ref, g, one).wait()


def pack(core, selected, queries, key_blocks, value_blocks):
    kv_count, block, kv_width = key_blocks.shape
    groups = kv_width // HD
    half_blocks, row_count, feat_width = queries.shape
    piece = block // half_blocks
    tall = kv_count * piece + feat_width // kv_width * row_count
    cut = (kv_count, half_blocks, piece, kv_width)
    scalars = pl.BlockSpec(memory_space=pltpu.SMEM)
    away = pl.BlockSpec(memory_space=pltpu.HBM)
    count = selected.shape[0] * (selected.shape[1] + 1)
    return pl.pallas_call(
        pack_kernel,
        out_shape=(
            jax.ShapeDtypeStruct((half_blocks, groups, tall, HD), queries.dtype),
            jax.ShapeDtypeStruct((count,), jnp.int32),
        ),
        in_specs=[scalars, scalars, away, away, away],
        out_specs=(pl.BlockSpec(memory_space=pltpu.VMEM), scalars),
        scratch_shapes=[
            pltpu.VMEM(queries.shape, queries.dtype),
            pltpu.SemaphoreType.DMA(()),
            pltpu.SemaphoreType.DMA((groups, kv_count)),
        ],
        compiler_params=pltpu.CompilerParams(vmem_limit_bytes=32 * 2**20),
        name="pack",
    )(
        core[None],
        *(
            pltpu.with_memory_space_constraint(array, pltpu.HBM)
            for array in (selected.T, queries, key_blocks.reshape(cut), value_blocks.reshape(cut))
        ),
    )


def pick_kernel(index_ref, table_ref, out_ref):
    def body(step, carry):
        for inner in range(8):
            place = step * 8 + inner
            out_ref[place] = table_ref[index_ref[place]]
        return carry

    lax.fori_loop(0, out_ref.shape[0] // 8, body, 0)


def pick(index, table):
    count = index.shape[0]
    return pl.pallas_call(
        pick_kernel,
        out_shape=jax.ShapeDtypeStruct((count,) + table.shape[1:], table.dtype),
        in_specs=[
            pl.BlockSpec(memory_space=pltpu.SMEM),
            pl.BlockSpec(memory_space=pltpu.VMEM),
        ],
        out_specs=pl.BlockSpec(memory_space=pltpu.VMEM),
        compiler_params=pltpu.CompilerParams(vmem_limit_bytes=32 * 2**20),
        name="pick",
    )(index, table)


def attend_kernel(row_count, parts, q_ref, kv_ref, out_ref, keys, values):
    spots, _, width, piece, _ = kv_ref.shape
    own_keys = spots * piece
    _, groups, rows_each, _ = out_ref.shape
    lead = q_ref.shape[2] - rows_each
    holders = spots * groups // parts
    per_group = spots // holders
    rows = holders * rows_each
    factor = math.log2(math.e) / math.sqrt(HD)
    nt = (((1,), (1,)), ((), ()))
    for j in range(width):
        place = pl.ds(j * own_keys, own_keys)
        keys[place] = kv_ref[:, 0, j].reshape(own_keys, HD)
        values[place, :HD] = kv_ref[:, 1, j].reshape(own_keys, HD)
    values[:, HD:] = jnp.ones((width * own_keys, HD), jnp.bfloat16)

    def steps(part):
        held = pl.ds(part % per_group * holders, holders)
        pair = part // per_group
        asked = q_ref[held, pair, lead:].reshape(rows, HD)
        seen = min(own_keys, -(-(part + 1) * holders * row_count // 128) * 128)
        spans = [(0, seen)] + [(j * own_keys, own_keys) for j in range(1, width)]
        scores = [
            lax.dot_general(asked, keys[pl.ds(*span)], nt, preferred_element_type=jnp.float32)
            for span in spans
        ]
        row = lax.broadcasted_iota(jnp.int32, (rows, 1), 0)
        token = (part * holders + row // rows_each) * row_count + row % row_count
        key = lax.broadcasted_iota(jnp.int32, (1, seen), 1)
        scores[0] = jnp.where(key <= token, scores[0], -jnp.inf)
        yield
        best = functools.reduce(jnp.maximum, [jnp.max(s, axis=1, keepdims=True) for s in scores])
        yield
        mixed = jnp.zeros((rows, 2 * HD), jnp.float32)
        for score, span in zip(scores, spans):
            weights = jnp.exp2((score - best) * factor).astype(jnp.bfloat16)
            mixed += jnp.dot(weights, values[pl.ds(*span)], preferred_element_type=jnp.float32)
        result = mixed[:, :HD] / mixed[:, HD:]
        out_ref[held, pair] = result.astype(out_ref.dtype).reshape(holders, rows_each, HD)
        yield

    running = [steps(part) for part in range(parts)]
    for _ in range(3):
        for one in running:
            next(one)


def attend(arrived, pieces, row_count, rows_each):
    spots, _, width, piece, _ = pieces.shape
    parts = 8
    whole = jax.ShapeDtypeStruct(arrived.shape[:2] + (rows_each, HD), jnp.bfloat16)
    near = pl.BlockSpec(memory_space=pltpu.VMEM)
    return pl.pallas_call(
        functools.partial(attend_kernel, row_count, parts),
        out_shape=whole,
        in_specs=[near, near],
        out_specs=near,
        scratch_shapes=[
            pltpu.VMEM((width * spots * piece, HD), jnp.bfloat16),
            pltpu.VMEM((width * spots * piece, 2 * HD), jnp.bfloat16),
        ],
        compiler_params=pltpu.CompilerParams(vmem_limit_bytes=48 * 2**20),
        name="attend",
    )(
        pltpu.with_memory_space_constraint(arrived, pltpu.VMEM),
        pltpu.with_memory_space_constraint(pieces, pltpu.VMEM),
    )


def unpack_kernel(back_ref, out_ref):
    row_count = out_ref.shape[1]
    _, groups, rows_each, _ = back_ref.shape
    heads = rows_each // row_count
    for g in range(groups):
        for head in range(heads):
            at = (g * heads + head) * HD
            rows = pl.ds(head * row_count, row_count)
            out_ref[:, :, at : at + HD] = back_ref[:, g, rows]


def unpack(back, shape):
    near = pl.BlockSpec(memory_space=pltpu.VMEM)
    return pl.pallas_call(
        unpack_kernel,
        out_shape=jax.ShapeDtypeStruct(shape, back.dtype),
        in_specs=[near],
        out_specs=near,
        name="unpack",
    )(pltpu.with_memory_space_constraint(back, pltpu.VMEM))


def local(queries, key_blocks, value_blocks, selected):
    core = lax.axis_index("c")
    half_blocks, row_count, feat_width = queries.shape
    kv_count, block, kv_width = key_blocks.shape
    heads = feat_width // kv_width
    pair_size = lax.axis_size(PAIR)
    piece = block // half_blocks
    width = selected.shape[1] + 1
    parcels, place = pack(core, selected, queries, key_blocks, value_blocks)
    laid = parcels.shape
    arrived = exchange(parcels.reshape((-1,) + laid[2:]), SPREAD)
    table = arrived.reshape(-1, piece, HD)
    sent = pick(place, pltpu.with_memory_space_constraint(table, pltpu.VMEM))
    pieces = exchange(sent.reshape(pair_size, width * piece, HD), PAIR)
    pieces = pieces.reshape(half_blocks, 2, width, piece, HD)
    done = attend(arrived.reshape(laid), pieces, row_count, heads * row_count)
    back = exchange(done.reshape((-1,) + done.shape[2:]), SPREAD)
    return unpack(back.reshape(done.shape), queries.shape)


def solution(mesh):
    z_pairs = 4
    ctx_size, cores = mesh.devices.shape
    plane = 4
    fine = mesh.devices.reshape(z_pairs, ctx_size // (z_pairs * plane * plane), plane, plane, cores)
    fine_mesh = Mesh(fine, ("zp", "zl", "x", "y", "c"))
    in_specs = (P("c", CTX, None), P(CTX, None, None), P(CTX, None, None), P())
    out_specs = P("c", CTX, None)
    return jax.shard_map(
        local, mesh=fine_mesh, in_specs=in_specs, out_specs=out_specs, check_vma=False
    )
```

```python
import functools
import math

import jax
import jax.numpy as jnp
from jax import lax
from jax.experimental import pallas as pl
from jax.experimental.pallas import tpu as pltpu
from jax.sharding import Mesh, PartitionSpec as P

HD = 128
CTX = ("zp", "zl", "x", "y")
SPREAD = ("zl", "x", "y", "zp")
PAIR = ("zl", "x", "y", "c")


def exchange(value, axes):
    return lax.all_to_all(value, axes, split_axis=0, concat_axis=0, tiled=True)


def pack_kernel(
    core_ref, chosen_ref, q_ref, k_ref, v_ref, out_ref, place_ref, asked, q_sem, in_sems
):
    kv_count, spots, piece, kv_width = k_ref.shape
    _, row_count, feat_width = q_ref.shape
    groups = kv_width // HD
    heads = feat_width // kv_width

    def fetch(ref, g, one):
        return pltpu.make_async_copy(
            ref.at[one, :, :, pl.ds(g * HD, HD)],
            out_ref.at[:, g, pl.ds(one * piece, piece)],
            in_sems.at[g, one],
        )

    whole = pltpu.make_async_copy(q_ref, asked, q_sem)
    whole.start()
    for core, ref in enumerate((k_ref, v_ref)):

        @pl.when(core_ref[0] == core)
        def _():
            for g in range(groups):
                for one in range(kv_count):
                    fetch(ref, g, one).start()

    topk, block_total = chosen_ref.shape
    width = topk + 1
    in_parcel = out_ref.shape[2] // piece
    first_own = spots * groups * kv_count - block_total

    assert kv_count & (kv_count - 1) == 0 and spots & (spots - 1) == 0
    kv_bits, spot_bits = kv_count.bit_length() - 1, spots.bit_length() - 1

    def note(spot, carry):
        for half in range(2):
            asker = half * spots + spot
            named = [first_own + asker] + [chosen_ref[j, asker] for j in range(topk)]
            for j, target in enumerate(named):
                holder = lax.shift_right_logical(target, kv_bits)
                inner = lax.bitwise_and(target, kv_count - 1)
                pair = lax.shift_right_logical(holder, spot_bits)
                came = lax.bitwise_and(holder, spots - 1) * groups + pair
                place_ref[(spot * 2 + half) * width + j] = came * in_parcel + inner
        return carry

    lax.fori_loop(0, spots, note, 0)
    whole.wait()
    for g in range(groups):
        for head in range(heads):
            rows = pl.ds(kv_count * piece + head * row_count, row_count)
            at = (g * heads + head) * HD
            out_ref[:, g, rows] = asked[:, :, at : at + HD]
    for g in range(groups):
        for one in range(kv_count):
            fetch(k_ref, g, one).wait()


def pack(core, selected, queries, key_blocks, value_blocks):
    kv_count, block, kv_width = key_blocks.shape
    groups = kv_width // HD
    half_blocks, row_count, feat_width = queries.shape
    piece = block // half_blocks
    tall = kv_count * piece + feat_width // kv_width * row_count
    cut = (kv_count, half_blocks, piece, kv_width)
    scalars = pl.BlockSpec(memory_space=pltpu.SMEM)
    away = pl.BlockSpec(memory_space=pltpu.HBM)
    count = selected.shape[0] * (selected.shape[1] + 1)
    return pl.pallas_call(
        pack_kernel,
        out_shape=(
            jax.ShapeDtypeStruct((half_blocks, groups, tall, HD), queries.dtype),
            jax.ShapeDtypeStruct((count,), jnp.int32),
        ),
        in_specs=[scalars, scalars, away, away, away],
        out_specs=(pl.BlockSpec(memory_space=pltpu.VMEM), scalars),
        scratch_shapes=[
            pltpu.VMEM(queries.shape, queries.dtype),
            pltpu.SemaphoreType.DMA(()),
            pltpu.SemaphoreType.DMA((groups, kv_count)),
        ],
        compiler_params=pltpu.CompilerParams(vmem_limit_bytes=32 * 2**20),
        name="pack",
    )(
        core[None],
        *(
            pltpu.with_memory_space_constraint(array, pltpu.HBM)
            for array in (selected.T, queries, key_blocks.reshape(cut), value_blocks.reshape(cut))
        ),
    )


def pick_kernel(index_ref, table_ref, out_ref):
    def body(step, carry):
        for inner in range(8):
            place = step * 8 + inner
            out_ref[place] = table_ref[index_ref[place]]
        return carry

    lax.fori_loop(0, out_ref.shape[0] // 8, body, 0)


def pick(index, table):
    count = index.shape[0]
    return pl.pallas_call(
        pick_kernel,
        out_shape=jax.ShapeDtypeStruct((count,) + table.shape[1:], table.dtype),
        in_specs=[
            pl.BlockSpec(memory_space=pltpu.SMEM),
            pl.BlockSpec(memory_space=pltpu.VMEM),
        ],
        out_specs=pl.BlockSpec(memory_space=pltpu.VMEM),
        compiler_params=pltpu.CompilerParams(vmem_limit_bytes=32 * 2**20),
        name="pick",
    )(index, table)


def attend_kernel(row_count, parts, q_ref, kv_ref, out_ref, keys, values):
    spots, _, width, piece, _ = kv_ref.shape
    own_keys = spots * piece
    _, groups, rows_each, _ = out_ref.shape
    lead = q_ref.shape[2] - rows_each
    holders = spots * groups // parts
    per_group = spots // holders
    rows = holders * rows_each
    factor = math.log2(math.e) / math.sqrt(HD)
    nt = (((1,), (1,)), ((), ()))
    for j in range(width):
        place = pl.ds(j * own_keys, own_keys)
        keys[place] = kv_ref[:, 0, j].reshape(own_keys, HD)
        values[place, :HD] = kv_ref[:, 1, j].reshape(own_keys, HD)
    values[:, HD:] = jnp.ones((width * own_keys, HD), jnp.bfloat16)

    def steps(part):
        held = pl.ds(part % per_group * holders, holders)
        pair = part // per_group
        asked = q_ref[held, pair, lead:].reshape(rows, HD)
        seen = min(own_keys, -(-(part + 1) * holders * row_count // 128) * 128)
        spans = [(0, seen)] + [(j * own_keys, own_keys) for j in range(1, width)]
        scores = [
            lax.dot_general(asked, keys[pl.ds(*span)], nt, preferred_element_type=jnp.float32)
            for span in spans
        ]
        row = lax.broadcasted_iota(jnp.int32, (rows, 1), 0)
        token = (part * holders + row // rows_each) * row_count + row % row_count
        key = lax.broadcasted_iota(jnp.int32, (1, seen), 1)
        scores[0] = jnp.where(key <= token, scores[0], -jnp.inf)
        yield
        best = functools.reduce(jnp.maximum, [jnp.max(s, axis=1, keepdims=True) for s in scores])
        yield
        mixed = jnp.zeros((rows, 2 * HD), jnp.float32)
        for score, span in zip(scores, spans):
            weights = jnp.exp2((score - best) * factor).astype(jnp.bfloat16)
            mixed += jnp.dot(weights, values[pl.ds(*span)], preferred_element_type=jnp.float32)
        result = mixed[:, :HD] / mixed[:, HD:]
        out_ref[held, pair] = result.astype(out_ref.dtype).reshape(holders, rows_each, HD)
        yield

    running = [steps(part) for part in range(parts)]
    for _ in range(3):
        for one in running:
            next(one)


def attend(arrived, pieces, row_count, rows_each):
    spots, _, width, piece, _ = pieces.shape
    parts = 8
    whole = jax.ShapeDtypeStruct(arrived.shape[:2] + (rows_each, HD), jnp.bfloat16)
    near = pl.BlockSpec(memory_space=pltpu.VMEM)
    return pl.pallas_call(
        functools.partial(attend_kernel, row_count, parts),
        out_shape=whole,
        in_specs=[near, near],
        out_specs=near,
        scratch_shapes=[
            pltpu.VMEM((width * spots * piece, HD), jnp.bfloat16),
            pltpu.VMEM((width * spots * piece, 2 * HD), jnp.bfloat16),
        ],
        compiler_params=pltpu.CompilerParams(vmem_limit_bytes=48 * 2**20),
        name="attend",
    )(
        pltpu.with_memory_space_constraint(arrived, pltpu.VMEM),
        pltpu.with_memory_space_constraint(pieces, pltpu.VMEM),
    )


def unpack_kernel(back_ref, out_ref):
    row_count = out_ref.shape[1]
    _, groups, rows_each, _ = back_ref.shape
    heads = rows_each // row_count
    for g in range(groups):
        for head in range(heads):
            at = (g * heads + head) * HD
            rows = pl.ds(head * row_count, row_count)
            out_ref[:, :, at : at + HD] = back_ref[:, g, rows]


def unpack(back, shape):
    near = pl.BlockSpec(memory_space=pltpu.VMEM)
    return pl.pallas_call(
        unpack_kernel,
        out_shape=jax.ShapeDtypeStruct(shape, back.dtype),
        in_specs=[near],
        out_specs=near,
        name="unpack",
    )(pltpu.with_memory_space_constraint(back, pltpu.VMEM))


def local(queries, key_blocks, value_blocks, selected):
    core = lax.axis_index("c")
    half_blocks, row_count, feat_width = queries.shape
    kv_count, block, kv_width = key_blocks.shape
    heads = feat_width // kv_width
    pair_size = lax.axis_size(PAIR)
    piece = block // half_blocks
    width = selected.shape[1] + 1
    parcels, place = pack(core, selected, queries, key_blocks, value_blocks)
    laid = parcels.shape
    arrived = exchange(parcels.reshape((-1,) + laid[2:]), SPREAD)
    table = arrived.reshape(-1, piece, HD)
    sent = pick(place, pltpu.with_memory_space_constraint(table, pltpu.VMEM))
    pieces = exchange(sent.reshape(pair_size, width * piece, HD), PAIR)
    pieces = pieces.reshape(half_blocks, 2, width, piece, HD)
    done = attend(arrived.reshape(laid), pieces, row_count, heads * row_count)
    back = exchange(done.reshape((-1,) + done.shape[2:]), SPREAD)
    return unpack(back.reshape(done.shape), queries.shape)


def solution(mesh):
    z_pairs = 4
    ctx_size, cores = mesh.devices.shape
    plane = 4
    fine = mesh.devices.reshape(z_pairs, ctx_size // (z_pairs * plane * plane), plane, plane, cores)
    fine_mesh = Mesh(fine, ("zp", "zl", "x", "y", "c"))
    in_specs = (P("c", CTX, None), P(CTX, None, None), P(CTX, None, None), P())
    out_specs = P("c", CTX, None)
    return jax.shard_map(
        local, mesh=fine_mesh, in_specs=in_specs, out_specs=out_specs, check_vma=False
    )
```

```python
import functools
import math

import jax
import jax.numpy as jnp
from jax import lax
from jax.experimental import pallas as pl
from jax.experimental.pallas import tpu as pltpu
from jax.sharding import Mesh, PartitionSpec as P

HD = 128
CTX = ("zp", "zl", "x", "y")
SPREAD = ("zl", "x", "y", "zp")
PAIR = ("zl", "x", "y", "c")


def exchange(value, axes):
    return lax.all_to_all(value, axes, split_axis=0, concat_axis=0, tiled=True)


def pack_kernel(
    core_ref, chosen_ref, q_ref, k_ref, v_ref, out_ref, place_ref, asked, q_sem, in_sems
):
    kv_count, spots, piece, kv_width = k_ref.shape
    _, row_count, feat_width = q_ref.shape
    groups = kv_width // HD
    heads = feat_width // kv_width

    def fetch(ref, g, one):
        return pltpu.make_async_copy(
            ref.at[one, :, :, pl.ds(g * HD, HD)],
            out_ref.at[:, g, pl.ds(one * piece, piece)],
            in_sems.at[g, one],
        )

    whole = pltpu.make_async_copy(q_ref, asked, q_sem)
    for core, ref in enumerate((k_ref, v_ref)):

        @pl.when(core_ref[0] == core)
        def _():
            for g in range(groups):
                for one in range(kv_count):
                    fetch(ref, g, one).start()

    whole.start()
    topk, block_total = chosen_ref.shape
    width = topk + 1
    in_parcel = out_ref.shape[2] // piece
    first_own = spots * groups * kv_count - block_total

    assert kv_count & (kv_count - 1) == 0 and spots & (spots - 1) == 0
    kv_bits, spot_bits = kv_count.bit_length() - 1, spots.bit_length() - 1

    def note(spot, carry):
        for half in range(2):
            asker = half * spots + spot
            named = [first_own + asker] + [chosen_ref[j, asker] for j in range(topk)]
            for j, target in enumerate(named):
                holder = lax.shift_right_logical(target, kv_bits)
                inner = lax.bitwise_and(target, kv_count - 1)
                pair = lax.shift_right_logical(holder, spot_bits)
                came = lax.bitwise_and(holder, spots - 1) * groups + pair
                place_ref[(spot * 2 + half) * width + j] = came * in_parcel + inner
        return carry

    lax.fori_loop(0, spots, note, 0)
    whole.wait()
    for g in range(groups):
        for head in range(heads):
            rows = pl.ds(kv_count * piece + head * row_count, row_count)
            at = (g * heads + head) * HD
            out_ref[:, g, rows] = asked[:, :, at : at + HD]
    for g in range(groups):
        for one in range(kv_count):
            fetch(k_ref, g, one).wait()


def pack(core, selected, queries, key_blocks, value_blocks):
    kv_count, block, kv_width = key_blocks.shape
    groups = kv_width // HD
    half_blocks, row_count, feat_width = queries.shape
    piece = block // half_blocks
    tall = kv_count * piece + feat_width // kv_width * row_count
    cut = (kv_count, half_blocks, piece, kv_width)
    scalars = pl.BlockSpec(memory_space=pltpu.SMEM)
    away = pl.BlockSpec(memory_space=pltpu.HBM)
    count = selected.shape[0] * (selected.shape[1] + 1)
    return pl.pallas_call(
        pack_kernel,
        out_shape=(
            jax.ShapeDtypeStruct((half_blocks, groups, tall, HD), queries.dtype),
            jax.ShapeDtypeStruct((count,), jnp.int32),
        ),
        in_specs=[scalars, scalars, away, away, away],
        out_specs=(pl.BlockSpec(memory_space=pltpu.VMEM), scalars),
        scratch_shapes=[
            pltpu.VMEM(queries.shape, queries.dtype),
            pltpu.SemaphoreType.DMA(()),
            pltpu.SemaphoreType.DMA((groups, kv_count)),
        ],
        compiler_params=pltpu.CompilerParams(vmem_limit_bytes=32 * 2**20),
        name="pack",
    )(
        core[None],
        *(
            pltpu.with_memory_space_constraint(array, pltpu.HBM)
            for array in (selected.T, queries, key_blocks.reshape(cut), value_blocks.reshape(cut))
        ),
    )


def pick_kernel(index_ref, table_ref, out_ref):
    def body(step, carry):
        for inner in range(32):
            place = step * 32 + inner
            out_ref[place] = table_ref[index_ref[place]]
        return carry

    lax.fori_loop(0, out_ref.shape[0] // 32, body, 0)


def pick(index, table):
    count = index.shape[0]
    return pl.pallas_call(
        pick_kernel,
        out_shape=jax.ShapeDtypeStruct((count,) + table.shape[1:], table.dtype),
        in_specs=[
            pl.BlockSpec(memory_space=pltpu.SMEM),
            pl.BlockSpec(memory_space=pltpu.VMEM),
        ],
        out_specs=pl.BlockSpec(memory_space=pltpu.VMEM),
        compiler_params=pltpu.CompilerParams(vmem_limit_bytes=32 * 2**20),
        name="pick",
    )(index, table)


def attend_kernel(row_count, parts, q_ref, kv_ref, out_ref, keys, values):
    spots, _, width, piece, _ = kv_ref.shape
    own_keys = spots * piece
    _, groups, rows_each, _ = out_ref.shape
    lead = q_ref.shape[2] - rows_each
    holders = spots * groups // parts
    per_group = spots // holders
    rows = holders * rows_each
    factor = math.log2(math.e) / math.sqrt(HD)
    nt = (((1,), (1,)), ((), ()))
    for j in range(width):
        place = pl.ds(j * own_keys, own_keys)
        keys[place] = kv_ref[:, 0, j].reshape(own_keys, HD)
        values[place, :HD] = kv_ref[:, 1, j].reshape(own_keys, HD)
    values[:, HD:] = jnp.ones((width * own_keys, HD), jnp.bfloat16)

    def steps(part):
        held = pl.ds(part % per_group * holders, holders)
        pair = part // per_group
        asked = q_ref[held, pair, lead:].reshape(rows, HD)
        seen = min(own_keys, -(-(part + 1) * holders * row_count // 128) * 128)
        spans = [(0, seen)] + [(j * own_keys, own_keys) for j in range(1, width)]
        scores = [
            lax.dot_general(asked, keys[pl.ds(*span)], nt, preferred_element_type=jnp.float32)
            for span in spans
        ]
        row = lax.broadcasted_iota(jnp.int32, (rows, 1), 0)
        token = (part * holders + row // rows_each) * row_count + row % row_count
        key = lax.broadcasted_iota(jnp.int32, (1, seen), 1)
        scores[0] = jnp.where(key <= token, scores[0], -jnp.inf)
        yield
        best = functools.reduce(jnp.maximum, [jnp.max(s, axis=1, keepdims=True) for s in scores])
        yield
        mixed = jnp.zeros((rows, 2 * HD), jnp.float32)
        for score, span in zip(scores, spans):
            weights = jnp.exp2((score - best) * factor).astype(jnp.bfloat16)
            mixed += jnp.dot(weights, values[pl.ds(*span)], preferred_element_type=jnp.float32)
        result = mixed[:, :HD] / mixed[:, HD:]
        out_ref[held, pair] = result.astype(out_ref.dtype).reshape(holders, rows_each, HD)
        yield

    running = [steps(part) for part in range(parts)]
    for _ in range(3):
        for one in running:
            next(one)


def attend(arrived, pieces, row_count, rows_each):
    spots, _, width, piece, _ = pieces.shape
    parts = 8
    whole = jax.ShapeDtypeStruct(arrived.shape[:2] + (rows_each, HD), jnp.bfloat16)
    near = pl.BlockSpec(memory_space=pltpu.VMEM)
    return pl.pallas_call(
        functools.partial(attend_kernel, row_count, parts),
        out_shape=whole,
        in_specs=[near, near],
        out_specs=near,
        scratch_shapes=[
            pltpu.VMEM((width * spots * piece, HD), jnp.bfloat16),
            pltpu.VMEM((width * spots * piece, 2 * HD), jnp.bfloat16),
        ],
        compiler_params=pltpu.CompilerParams(vmem_limit_bytes=48 * 2**20),
        name="attend",
    )(
        pltpu.with_memory_space_constraint(arrived, pltpu.VMEM),
        pltpu.with_memory_space_constraint(pieces, pltpu.VMEM),
    )


def unpack_kernel(back_ref, out_ref):
    row_count = out_ref.shape[1]
    _, groups, rows_each, _ = back_ref.shape
    heads = rows_each // row_count
    for g in range(groups):
        for head in range(heads):
            at = (g * heads + head) * HD
            rows = pl.ds(head * row_count, row_count)
            out_ref[:, :, at : at + HD] = back_ref[:, g, rows]


def unpack(back, shape):
    near = pl.BlockSpec(memory_space=pltpu.VMEM)
    return pl.pallas_call(
        unpack_kernel,
        out_shape=jax.ShapeDtypeStruct(shape, back.dtype),
        in_specs=[near],
        out_specs=near,
        name="unpack",
    )(pltpu.with_memory_space_constraint(back, pltpu.VMEM))


def local(queries, key_blocks, value_blocks, selected):
    core = lax.axis_index("c")
    half_blocks, row_count, feat_width = queries.shape
    kv_count, block, kv_width = key_blocks.shape
    heads = feat_width // kv_width
    pair_size = lax.axis_size(PAIR)
    piece = block // half_blocks
    width = selected.shape[1] + 1
    parcels, place = pack(core, selected, queries, key_blocks, value_blocks)
    laid = parcels.shape
    arrived = exchange(parcels.reshape((-1,) + laid[2:]), SPREAD)
    table = arrived.reshape(-1, piece, HD)
    sent = pick(place, pltpu.with_memory_space_constraint(table, pltpu.VMEM))
    pieces = exchange(sent.reshape(pair_size, width * piece, HD), PAIR)
    pieces = pieces.reshape(half_blocks, 2, width, piece, HD)
    done = attend(arrived.reshape(laid), pieces, row_count, heads * row_count)
    back = exchange(done.reshape((-1,) + done.shape[2:]), SPREAD)
    return unpack(back.reshape(done.shape), queries.shape)


def solution(mesh):
    z_pairs = 4
    ctx_size, cores = mesh.devices.shape
    plane = 4
    fine = mesh.devices.reshape(z_pairs, ctx_size // (z_pairs * plane * plane), plane, plane, cores)
    fine_mesh = Mesh(fine, ("zp", "zl", "x", "y", "c"))
    in_specs = (P("c", CTX, None), P(CTX, None, None), P(CTX, None, None), P())
    out_specs = P("c", CTX, None)
    return jax.shard_map(
        local, mesh=fine_mesh, in_specs=in_specs, out_specs=out_specs, check_vma=False
    )
```
